256 devices in a mesh: seq: 32 (over x, y, core), head: 8 (over z).
Axes of the slice: x: 4, y: 4, z: 8, core: 2. Of those that a mesh axis runs over, the one named last changes fastest.
Arguments:
- queries: float32 [16384, 1024], P('seq', 'head'), may hold values from -6 to 6
- keys: float32 [16384, 1024], P('seq', 'head'), may hold values from -5 to 5
- values: float32 [16384, 1024], P('seq', 'head'), may hold values from -15 to 15
- gain: float32 [1024], P('head'), may hold values from 0.1 to 1.9
- ridge: float32 [8], P('head'), may hold values from 0.01 to 0.1
- prior_gram: float32 [8, 128, 128], P('head'), as said below
- prior_cross: float32 [8, 128, 128], P('head')
- cotangent: float32 [16384, 1024], P('seq', 'head'), may hold values from -6 to 6
Outputs:
- normed: float32 [16384, 1024], P('seq', 'head')
- grad_queries: float32 [16384, 1024], P('seq', 'head')
- grad_keys: float32 [16384, 1024], P('seq', 'head')
- grad_values: float32 [16384, 1024], P('seq', 'head')
The draws below stay inside these ranges and needn't reach their ends.
Inputs may be any that keep to these rules, and one draw needn't show every extreme that they name: `prior_gram`: each head's matrix is symmetric positive definite.
All inputs are finite; a program needn't handle non-finite values.
Results may differ from the reference program's by a relative error of at most 0.0003.
Values sent between devices are 32-bit elements; how exact they have to be, the bound alone decides.
A program may use at most 64 MiB of HBM per device.

```python
import math
import jax
import jax.numpy as jnp
from jax import lax

DH = 128
ITERS = 8
TOK_DEV = 512
HEADS = 8
FEATURES = 1024
TOKENS = 16384


def draw_keys(key, part):
    first, second = jax.random.split(jax.random.fold_in(key, 11), 2)
    column = jnp.exp(jax.random.uniform(first, (FEATURES,), jnp.float32, jnp.log(0.2), 0.0))
    base = jnp.clip(jax.random.normal(second, (TOKENS, FEATURES), jnp.float32), -5.0, 5.0)
    return jnp.clip(base * column, -5.0, 5.0).astype(jnp.float32)


def draw_values(key, part):
    second = jax.random.fold_in(jax.random.fold_in(key, 23), 1)
    heads_of = (jnp.arange(FEATURES) // DH).astype(jnp.float32)
    ramp = 1.0 + 2.0 * heads_of / max(HEADS - 1, 1)
    base = jnp.clip(jax.random.normal(second, (TOKENS, FEATURES), jnp.float32), -5.0, 5.0)
    return (base * ramp).astype(jnp.float32)


def prior_pair(key):
    first, second, third = jax.random.split(jax.random.fold_in(key, 37), 3)
    column = jnp.exp(jax.random.uniform(first, (HEADS, 1, DH), jnp.float32, jnp.log(0.2), 0.0))
    basis = jnp.clip(jax.random.normal(second, (HEADS, 4 * DH, DH), jnp.float32), -5.0, 5.0) * column
    filler = jnp.clip(jax.random.normal(third, (HEADS, 4 * DH, DH), jnp.float32), -5.0, 5.0)
    gram = jnp.einsum('hri,hrj->hij', basis, basis, precision=lax.Precision.HIGHEST)
    cross = jnp.einsum('hri,hrj->hij', basis, filler, precision=lax.Precision.HIGHEST)
    return (gram, cross)


def draw_prior_gram(key, part):
    return prior_pair(key)[0].astype(jnp.float32)


def draw_prior_cross(key, part):
    return prior_pair(key)[1].astype(jnp.float32)


def block_scale(rng, dims, shards, low, high):
    level = 1.0
    for axis_at, parts in shards:
        heights = jax.random.uniform(jax.random.fold_in(jax.random.fold_in(rng, 6), axis_at), (parts,), jnp.float32, low / len(shards), high / len(shards))
        level = level * jnp.repeat(jnp.exp(heights), dims[axis_at] // parts).reshape((-1,) + (1,) * (len(dims) - 1 - axis_at))
    return level


def bell_draw(stream_key, dims, scale, bound, cuts=(), held_as=jnp.bfloat16):
    values = jax.random.normal(stream_key, dims, jnp.float32) * scale
    if len(cuts) > 0:
        values = block_scale(stream_key, dims, cuts, -0.22, 0.18) * values
    return jnp.clip(values, min=-bound, max=bound).astype(held_as)


def setup_inputs(seed: int = 0) -> dict:
    key_of = jax.random.split(jax.random.key(seed), 9)
    return {
        "queries": bell_draw(key_of[0], (TOKENS, FEATURES), 1.0, 6.0, ((0, 32), (1, 8)), jnp.float32),
        "keys": draw_keys(jax.random.fold_in(key_of[8], 71), 0),
        "values": draw_values(jax.random.fold_in(key_of[8], 71), 0),
        "gain": jnp.clip(1.0 + 0.18 * jax.random.normal(key_of[3], (FEATURES,), jnp.float32), 0.1, 1.9),
        "ridge": jnp.clip(jnp.exp(math.log(0.1) - 2.3025851 * jax.random.uniform(key_of[4], (HEADS,), jnp.float32) ** block_scale(key_of[4], (HEADS,), ((0, 8),), -0.2, 0.2)), 0.01, 0.1),
        "prior_gram": draw_prior_gram(jax.random.fold_in(key_of[8], 71), 0),
        "prior_cross": draw_prior_cross(jax.random.fold_in(key_of[8], 71), 0),
        "cotangent": bell_draw(key_of[7], (TOKENS, FEATURES), 1.0, 6.0, ((0, 32), (1, 8)), jnp.float32),
    }


epsilon = 1e-06

def block_forward(query, keyset, valueset, start_gram, start_cross, ridge_value, first_row):
    highest = lax.Precision.HIGHEST
    count = query.shape[0]
    places = jnp.arange(count)
    causal = (places[None, :] <= places[:, None]).astype(jnp.float32)
    damping = ridge_value * (first_row + places + 1).astype(jnp.float32)[:, None]

    def apply_system(search):
        inner = jnp.dot(search, keyset.T, precision=highest) * causal
        return jnp.dot(search, start_gram, precision=highest) + jnp.dot(inner, keyset, precision=highest) + damping * search

    def cg_step(carry, unused):
        solution, residual, search, squared = carry
        image = apply_system(search)
        alpha = squared / lax.optimization_barrier(jnp.sum(search * image, axis=1, keepdims=True))
        solution = solution + alpha * search
        residual = residual - alpha * image
        squared_next = lax.optimization_barrier(jnp.sum(residual * residual, axis=1, keepdims=True))
        search = residual + squared_next / squared * search
        return ((solution, residual, search, squared_next), None)
    squared = lax.optimization_barrier(jnp.sum(query * query, axis=1, keepdims=True))
    start = (jnp.zeros_like(query), query, query, squared)
    (solution, _, _, _), _ = lax.scan(cg_step, start, None, length=ITERS)
    inner = jnp.dot(solution, keyset.T, precision=highest) * causal
    return jnp.dot(solution, start_cross, precision=highest) + jnp.dot(inner, valueset, precision=highest)

def head_output(packed):
    head_q, head_k, head_v, ridge_value, init_gram, init_cross = packed
    highest = lax.Precision.HIGHEST
    checked = jax.checkpoint(block_forward)

    def advance(carry, block):
        gram, cross, first_row = carry
        query, keyset, valueset = block
        output = checked(query, keyset, valueset, gram, cross, ridge_value, first_row)
        gram = gram + jnp.dot(keyset.T, keyset, precision=highest)
        cross = cross + jnp.dot(keyset.T, valueset, precision=highest)
        return ((gram, cross, first_row + TOK_DEV), output)
    start_state = (init_gram, init_cross, jnp.zeros((), jnp.int32))
    _, outputs = lax.scan(advance, start_state, (head_q, head_k, head_v))
    return outputs

def layer_forward(queries, keys, values, gain, ridge, prior_gram, prior_cross):
    blocks = TOKENS // TOK_DEV

    def by_head(array):
        return array.reshape(TOKENS, HEADS, DH).transpose(1, 0, 2).reshape(HEADS, blocks, TOK_DEV, DH)
    outputs = lax.map(head_output, (by_head(queries), by_head(keys), by_head(values), ridge, prior_gram, prior_cross))
    mixed = outputs.reshape(HEADS, TOKENS, DH).transpose(1, 0, 2).reshape(TOKENS, FEATURES)
    meansq = lax.optimization_barrier(jnp.mean(mixed * mixed, axis=1, keepdims=True))
    return mixed * lax.rsqrt(meansq + epsilon) * gain

def reference(queries, keys, values, gain, ridge, prior_gram, prior_cross, cotangent):

    def forward(first, second, third):
        return layer_forward(first, second, third, gain, ridge, prior_gram, prior_cross)
    normed, pullback = jax.vjp(forward, queries, keys, values)
    grad_queries, grad_keys, grad_values = pullback(cotangent)
    return (normed, grad_queries, grad_keys, grad_values)
```

```python
import functools

import jax
import jax.numpy as jnp
from jax import lax
from jax.experimental import pallas as pl
from jax.experimental.pallas import tpu as pltpu
from jax.sharding import PartitionSpec as P

DH = 128
ITERS = 8
CH = 128
epsilon = 1e-06

F32 = jnp.float32
BF16 = jnp.bfloat16
MESH = pl.DeviceIdType.MESH


def left(x):
    hi = x.astype(BF16)
    lo = (x - hi.astype(F32)).astype(BF16)
    return jnp.concatenate([hi, lo], axis=1)


def right(halves):
    return jnp.concatenate([halves, halves], axis=0)


def right_t(halves):
    hi, lo = halves[:, :CH], halves[:, CH:]
    return jnp.concatenate(
        [jnp.concatenate([hi, hi], axis=1), jnp.concatenate([lo, lo], axis=1)], axis=0
    )


def fold(out):
    return out[:, :CH] + out[:, CH:]


def mul(a, b):
    return fold(jnp.dot(a, right(b), preferred_element_type=F32))


def mul_t(pairs):
    a = jnp.concatenate([pair[0] for pair in pairs], axis=1)
    b = jnp.concatenate([right_t(pair[1]) for pair in pairs], axis=1)
    return fold(
        lax.dot_general(a, b, (((1,), (1,)), ((), ())), preferred_element_type=F32)
    )


def colsum(x):
    return jnp.sum(x, axis=0, keepdims=True)


def kernel(
    n_seq, n_head, features,
    q_hbm, k_hbm, v_hbm, gain_ref, ridge_ref, pg_hbm, pc_hbm, cot_hbm,
    normed_hbm, gq_hbm, gk_hbm, gv_hbm,
    q_in, k_in, v_in, cot_in, pg_in, pc_in,
    ak, kt, vl, vtl, cl, ctl, mg, mc, qt, ct,
    pf, wf, rf, pl_, sl, wbl, sbl, al, be, rrs, pws,
    xt, mx, sxl, syl, yl, xb, pb, rb, rrb, dsy, dcc,
    nat, o_normed, o_gq, o_gk, o_gv,
    src, recv1, buf2, recv2, stat, stat_in,
    in_sem, out_sem, s1, r1, s2, r2, hs, hr,
):
    me = lax.axis_index("seq")
    my_head = lax.axis_index("head")
    n_own = n_seq // 2
    pr = DH // n_own
    nch = k_in.shape[0] // CH
    mine = me // 2
    core = me - 2 * mine

    loads = []
    for at, (source, target) in enumerate(
        ((k_hbm, k_in), (v_hbm, v_in), (q_hbm, q_in), (pg_hbm.at[0], pg_in),
         (pc_hbm.at[0], pc_in), (cot_hbm, cot_in))
    ):
        copy = pltpu.make_async_copy(source, target, in_sem.at[at])
        copy.start()
        loads.append(copy)

    barrier = pltpu.get_barrier_semaphore()

    def greet_seq(turn, carry):
        pl.semaphore_signal(
            barrier, inc=1, device_id={"seq": lax.rem(me + turn, n_seq)}, device_id_type=MESH
        )
        return carry

    def greet_head(turn, carry):
        pl.semaphore_signal(
            barrier, inc=1, device_id={"head": lax.rem(my_head + turn, n_head)},
            device_id_type=MESH,
        )
        return carry

    lax.fori_loop(1, n_seq, greet_seq, 0)
    lax.fori_loop(1, n_head, greet_head, 0)

    def bytes_wait(ref, count, sem):
        view = ref.at[pl.ds(0, count)]
        pltpu.make_async_copy(view, view, sem).wait()

    def send_first(x, parity):
        def one(turn, carry):
            piece = lax.rem(mine + turn, n_own)
            owner = 2 * piece + parity

            @pl.when(owner != me)
            def _():
                pltpu.make_async_remote_copy(
                    src_ref=src.at[x, piece], dst_ref=recv1.at[x, me],
                    send_sem=s1.at[x], recv_sem=r1.at[x],
                    device_id={"seq": owner}, device_id_type=MESH,
                ).start()

            return carry

        lax.fori_loop(0, n_own, one, 0)

        @pl.when(core == parity)
        def _():
            recv1[x, me] = src[x, mine]

    def send_second(x, parity, reverse, base):
        @pl.when(core == parity)
        def _():
            bytes_wait(recv1.at[x], n_seq - 1, r1.at[x])
            if base is None:
                total = jnp.zeros((pr, DH), F32)
            else:
                total = base[pl.ds(pl.multiple_of(mine * pr, pr), pr), :]
            order = range(n_seq - 1, -1, -1) if reverse else range(n_seq)
            for device in order:
                buf2[x, device] = total
                total = total + recv1[x, device]

            def one(turn, carry):
                device = lax.rem(me + turn, n_seq)
                pltpu.make_async_remote_copy(
                    src_ref=buf2.at[x, device], dst_ref=recv2.at[x, mine],
                    send_sem=s2.at[x], recv_sem=r2.at[x],
                    device_id={"seq": device}, device_id_type=MESH,
                ).start()
                return carry

            lax.fori_loop(1, n_seq, one, 0)
            recv2[x, mine] = buf2[x, me]

    def finish(x, parity):
        @pl.when(core == parity)
        def _():
            bytes_wait(recv2.at[x], n_own - 1, r2.at[x])

        @pl.when(core != parity)
        def _():
            bytes_wait(recv2.at[x], n_own, r2.at[x])

        return recv2[x].reshape(DH, DH)

    def drain(x, parity):
        @pl.when(core == parity)
        def _():
            bytes_wait(src.at[x], n_own - 1, s1.at[x])
            bytes_wait(buf2.at[x], n_seq - 1, s2.at[x])

        @pl.when(core != parity)
        def _():
            bytes_wait(src.at[x], n_own, s1.at[x])

    rows = [pl.ds(c * CH, CH) for c in range(nch)]
    keep = (
        lax.broadcasted_iota(jnp.int32, (CH, CH), 0)
        <= lax.broadcasted_iota(jnp.int32, (CH, CH), 1)
    )
    lane = lax.broadcasted_iota(jnp.int32, (1, CH), 1)
    first_row = me * k_in.shape[0]
    damping = [
        ridge_ref[0] * (first_row + (c * CH + 1) + lane).astype(F32) for c in range(nch)
    ]

    loads[0].wait()
    total = jnp.zeros((DH, DH), F32)
    for c in range(nch):
        keys = k_in[rows[c], :]
        halves = left(keys)
        halves_t = left(keys.T)
        ak[c, DH:, :] = halves
        kt[c] = halves_t
        gram = mul(halves_t, halves)
        mg[c] = gram
        total = total + gram
    src[0] = total.reshape(n_own, pr, DH)
    pl.semaphore_wait(barrier, n_seq - 1 + n_head - 1)
    send_first(0, 0)

    loads[1].wait()
    total = jnp.zeros((DH, DH), F32)
    for c in range(nch):
        values = v_in[rows[c], :]
        halves = left(values)
        vl[c] = halves
        cross = mul(kt[c], halves)
        mc[c] = cross
        total = total + cross
    src[1] = total.reshape(n_own, pr, DH)
    send_first(1, 1)
    loads[3].wait()
    loads[4].wait()
    send_second(0, 0, False, pg_in)
    send_second(1, 1, False, pc_in)

    loads[2].wait()
    loads[5].wait()
    for c in range(nch):
        vtl[c] = left(v_in[rows[c], :].T)
        qt[c] = q_in[rows[c], :].T
        ct[c] = (cot_in[rows[c], :] * gain_ref[...]).T

    def apply_system(c, halves, search):
        both = fold(jnp.dot(ak[c], right(halves), preferred_element_type=F32))
        inner = left(jnp.where(keep, both[DH:], 0.0))
        return both[:DH] + mul(kt[c], inner) + damping[c] * search, inner

    gram = finish(0, 0)
    for c in range(nch):
        ak[c, :DH, :] = left(gram)
        if c + 1 < nch:
            gram = gram + mg[c]

    for c in range(nch):
        start = qt[c]
        pf[0, c] = start
        pl_[0, c] = left(start)
        rrs[0, c : c + 1, :] = colsum(start * start)
        xt[c] = jnp.zeros_like(start)

    def forward(step, carry):
        for c in range(nch):
            search = pf[step, c]
            image, inner = apply_system(c, pl_[step, c], search)
            wf[step, c] = image
            sl[step, c] = inner
            squared = rrs[step, c : c + 1, :]
            curve = colsum(search * image)
            alpha = squared / curve
            pws[step, c : c + 1, :] = curve
            al[step, c : c + 1, :] = alpha
            xt[c] = xt[c] + alpha * search
            before = qt[c]
            residual = before - alpha * image
            qt[c] = residual
            rf[step, c] = residual
            squared_next = colsum(residual * residual)
            beta = squared_next / squared
            be[step, c : c + 1, :] = beta
            rrs[step + 1, c : c + 1, :] = squared_next
            search = residual + beta * search
            pf[step + 1, c] = search
            pl_[step + 1, c] = left(search)
        return carry

    lax.fori_loop(0, ITERS, forward, 0)

    cross = finish(1, 1)
    for c in range(nch):
        cl[c] = left(cross)
        ctl[c] = left(cross.T)
        if c + 1 < nch:
            cross = cross + mc[c]
    for c in range(nch):
        halves = left(xt[c])
        inner = left(jnp.where(keep, mul(ak[c, DH:, :], halves), 0.0))
        sxl[c] = inner
        mixed = mul(ctl[c], halves) + mul(vtl[c], inner)
        mx[c] = mixed
        stat[c : c + 1, :] = colsum(mixed * mixed)
        stat[nch + c : nch + c + 1, :] = colsum(ct[c] * mixed)

    def send_stat(turn, carry):
        device = lax.rem(my_head + turn, n_head)
        pltpu.make_async_remote_copy(
            src_ref=stat, dst_ref=stat_in.at[my_head], send_sem=hs.at[0], recv_sem=hr.at[0],
            device_id={"head": device}, device_id_type=MESH,
        ).start()
        return carry

    lax.fori_loop(1, n_head, send_stat, 0)
    stat_in[my_head] = stat[...]
    bytes_wait(stat_in, n_head - 1, hr.at[0])
    sums = stat_in[0]
    for device in range(1, n_head):
        sums = sums + stat_in[device]
    inverse = lax.rsqrt(sums[:nch] / features + epsilon)
    pull = inverse * inverse * inverse * (sums[nch:] / features)

    total = jnp.zeros((DH, DH), F32)
    for c in range(nch):
        scale = inverse[c : c + 1, :]
        mixed = mx[c]
        o_normed[rows[c], :] = (mixed * scale).T * gain_ref[...]
        grad = left(scale * ct[c] - mixed * pull[c : c + 1, :])
        yl[c] = grad
        inner = left(jnp.where(keep, mul(vl[c], grad), 0.0))
        syl[c] = inner
        xb[c] = mul(cl[c], grad) + mul(kt[c], inner)
        part = mul_t([(left(xt[c]), grad)])
        dcc[c] = part
        total = total + part
    src[3] = total.reshape(n_own, pr, DH)
    send_first(3, 1)
    stores = [pltpu.make_async_copy(o_normed, normed_hbm, out_sem.at[0])]
    stores[0].start()

    last = ITERS - 1
    for c in range(nch):
        search, image, solution_bar = pf[last, c], wf[last, c], xb[c]
        alpha, curve = al[last, c : c + 1, :], pws[last, c : c + 1, :]
        alpha_bar = colsum(solution_bar * search)
        curve_bar = -alpha_bar * alpha / curve
        wbl[last, c] = left(curve_bar * search)
        halves = sl[last, c]
        sbl[last, c] = left(
            curve_bar * (halves[:, :CH].astype(F32) + halves[:, CH:].astype(F32))
        )
        pb[c] = alpha * solution_bar + 2.0 * curve_bar * image
        rb[c] = jnp.zeros((DH, CH), F32)
        rrb[c : c + 1, :] = alpha_bar / curve

    def backward(turn, carry):
        step = last - 1 - turn
        for c in range(nch):
            search, image, solution_bar = pf[step, c], wf[step, c], xb[c]
            alpha, curve = al[step, c : c + 1, :], pws[step, c : c + 1, :]
            beta, squared = be[step, c : c + 1, :], rrs[step, c : c + 1, :]
            search_bar = pb[c]
            beta_bar = colsum(search_bar * search) / squared
            next_bar = rrb[c : c + 1, :] + beta_bar
            residual_bar = rb[c] + search_bar + (2.0 * next_bar) * rf[step, c]
            alpha_bar = colsum(solution_bar * search - residual_bar * image)
            ratio = alpha_bar / curve
            curve_bar = -ratio * alpha
            image_bar = curve_bar * search - alpha * residual_bar
            halves = left(image_bar)
            wbl[step, c] = halves
            moved, inner = apply_system(c, halves, image_bar)
            sbl[step, c] = inner
            pb[c] = beta * search_bar + alpha * solution_bar + curve_bar * image + moved
            rb[c] = residual_bar
            rrb[c : c + 1, :] = ratio - beta_bar * beta
        return carry

    lax.fori_loop(0, last, backward, 0)

    total = jnp.zeros((DH, DH), F32)
    for c in range(nch):
        part = mul_t([(pl_[j, c], wbl[j, c]) for j in range(ITERS)])
        part = part + part.T
        dsy[c] = part
        total = total + part
    src[2] = total.reshape(n_own, pr, DH)
    send_first(2, 0)
    send_second(3, 1, True, None)

    for c in range(nch):
        first = q_in[rows[c], :].T
        grad = rb[c] + pb[c] + 2.0 * rrb[c : c + 1, :] * first
        o_gq[rows[c], :] = grad.T
    stores.append(pltpu.make_async_copy(o_gq, gq_hbm, out_sem.at[1]))
    stores[1].start()
    send_second(2, 0, True, None)
    for c in range(nch):
        pairs = [(syl[c], left(xt[c]))]
        for j in range(ITERS):
            pairs.append((sl[j, c], wbl[j, c]))
            pairs.append((sbl[j, c], pl_[j, c]))
        o_gk[rows[c], :] = mul_t(pairs)
        o_gv[rows[c], :] = mul_t([(sxl[c], yl[c])])

    cross = finish(3, 1)
    for c in range(nch - 1, -1, -1):
        halves = left(cross)
        o_gv[rows[c], :] += mul(ak[c, DH:, :], halves)
        o_gk[rows[c], :] += mul_t([(vl[c], halves)])
        cross = cross + dcc[c]
    stores.append(pltpu.make_async_copy(o_gv, gv_hbm, out_sem.at[3]))
    stores[2].start()
    gram = finish(2, 0)
    for c in range(nch - 1, -1, -1):
        o_gk[rows[c], :] += mul(ak[c, DH:, :], left(gram))
        gram = gram + dsy[c]
    stores.append(pltpu.make_async_copy(o_gk, gk_hbm, out_sem.at[2]))
    stores[3].start()

    bytes_wait(stat_in, n_head - 1, hs.at[0])
    drain(0, 0)
    drain(1, 1)
    drain(2, 0)
    drain(3, 1)
    for copy in stores:
        copy.wait()


def local(n_seq, n_head, queries, keys, values, gain, ridge, prior_gram, prior_cross, cotangent):
    rows, width = queries.shape
    nch = rows // CH
    n_own = n_seq // 2
    pr = DH // n_own
    anyspace = pl.BlockSpec(memory_space=pl.ANY)
    vmem = pl.BlockSpec(memory_space=pltpu.VMEM)
    smem = pl.BlockSpec(memory_space=pltpu.SMEM)
    tok = pltpu.VMEM((rows, DH), F32)
    square = pltpu.VMEM((DH, DH), F32)
    per_chunk = pltpu.VMEM((nch, DH, CH), F32)
    halves = pltpu.VMEM((nch, DH, 2 * CH), BF16)
    per_step = pltpu.VMEM((ITERS, nch, DH, CH), F32)
    step_halves = pltpu.VMEM((ITERS, nch, DH, 2 * CH), BF16)
    scal = pltpu.VMEM((ITERS + 1, nch, CH), F32)
    scratch = [
        tok, tok, tok, tok, square, square,
        pltpu.VMEM((nch, 2 * DH, 2 * CH), BF16), halves, halves, halves, halves, halves,
        per_chunk, per_chunk, per_chunk, per_chunk,
        pltpu.VMEM((ITERS + 1, nch, DH, CH), F32), per_step, per_step,
        pltpu.VMEM((ITERS + 1, nch, DH, 2 * CH), BF16), step_halves, step_halves, step_halves,
        scal, scal, scal, scal,
        per_chunk, per_chunk, halves, halves, halves, per_chunk, per_chunk, per_chunk,
        pltpu.VMEM((nch, CH), F32), per_chunk, per_chunk,
        tok, tok, tok, tok, tok,
        pltpu.VMEM((4, n_own, pr, DH), F32), pltpu.VMEM((4, n_seq, pr, DH), F32),
        pltpu.VMEM((4, n_seq, pr, DH), F32), pltpu.VMEM((4, n_own, pr, DH), F32),
        pltpu.VMEM((2 * nch, CH), F32), pltpu.VMEM((n_head, 2 * nch, CH), F32),
        pltpu.SemaphoreType.DMA((6,)), pltpu.SemaphoreType.DMA((4,)),
        pltpu.SemaphoreType.DMA((4,)), pltpu.SemaphoreType.DMA((4,)),
        pltpu.SemaphoreType.DMA((4,)), pltpu.SemaphoreType.DMA((4,)),
        pltpu.SemaphoreType.DMA((1,)), pltpu.SemaphoreType.DMA((1,)),
    ]
    shape = jax.ShapeDtypeStruct((rows, width), F32)
    return pl.pallas_call(
        functools.partial(kernel, n_seq, n_head, float(width * n_head)),
        out_shape=(shape, shape, shape, shape),
        in_specs=[anyspace, anyspace, anyspace, vmem, smem, anyspace, anyspace, anyspace],
        out_specs=(anyspace, anyspace, anyspace, anyspace),
        scratch_shapes=scratch,
        compiler_params=pltpu.CompilerParams(
            collective_id=0, has_side_effects=True, vmem_limit_bytes=60 * 1024 * 1024
        ),
    )(queries, keys, values, gain.reshape(1, width), ridge, prior_gram, prior_cross, cotangent)


def solution(mesh):
    in_specs = (
        P("seq", "head"),
        P("seq", "head"),
        P("seq", "head"),
        P("head"),
        P("head"),
        P("head", None, None),
        P("head", None, None),
        P("seq", "head"),
    )
    out_specs = (P("seq", "head"), P("seq", "head"), P("seq", "head"), P("seq", "head"))
    body = functools.partial(local, mesh.shape["seq"], mesh.shape["head"])
    return jax.shard_map(body, mesh=mesh, in_specs=in_specs, out_specs=out_specs, check_vma=False)
```

```python
import functools

import jax
import jax.numpy as jnp
from jax import lax
from jax.experimental import pallas as pl
from jax.experimental.pallas import tpu as pltpu
from jax.sharding import PartitionSpec as P

DH = 128
ITERS = 8
CH = 128
epsilon = 1e-06

F32 = jnp.float32
BF16 = jnp.bfloat16
MESH = pl.DeviceIdType.MESH


def left(x):
    hi = x.astype(BF16)
    lo = (x - hi.astype(F32)).astype(BF16)
    return jnp.concatenate([hi, lo], axis=1)


def right(halves):
    return jnp.concatenate([halves, halves], axis=0)


def fold(out):
    return out[:, :CH] + out[:, CH:]


def mul(a, b):
    return fold(jnp.dot(a, right(b), preferred_element_type=F32))


def mul_cat(pairs):
    a = jnp.concatenate([pair[0] for pair in pairs], axis=1)
    b = jnp.concatenate([right(pair[1]) for pair in pairs], axis=0)
    return fold(jnp.dot(a, b, preferred_element_type=F32))


def stack(parts):
    his = jnp.concatenate([part[:, :CH] for part in parts], axis=1)
    los = jnp.concatenate([part[:, CH:] for part in parts], axis=1)
    return jnp.concatenate([his, los], axis=0)


def mul_t(pairs):
    out = fold(
        lax.dot_general(
            stack([pair[0] for pair in pairs]), stack([pair[1] for pair in pairs]),
            (((1,), (1,)), ((), ())), preferred_element_type=F32,
        )
    )
    return out[:DH] + out[DH:]


def colsum(x):
    while x.shape[0] > 8:
        half = x.shape[0] // 2
        x = x[:half] + x[half:]
    for shift in (4, 2, 1):
        x = x + pltpu.roll(x, shift, 0)
    return x


def scaled(row, x):
    return (x.reshape(-1, 8, CH) * row).reshape(x.shape)


def interleave(makers, offsets):
    chains = [(maker, late) for maker, late in zip(makers, offsets)]
    turn = 0
    while chains:
        left_over = []
        for chain, late in chains:
            if turn < late or next(chain, True) is None:
                left_over.append((chain, late))
        chains = left_over
        turn += 1


def hops(offset):
    return (0, 1, 2, 1)[offset]


def kernel(
    n_seq, n_head, features,
    q_hbm, k_hbm, v_hbm, gain_hbm, ridge_hbm, pg_hbm, pc_hbm, cot_hbm,
    o_normed, o_gq, o_gk, o_gv,
    q_in, k_in, v_in, cot_in, pg_in, pc_in, gain_in, ridge_in,
    ak, kt, vl, vtl, cl, ctl, mg, mc, qt, ct,
    pf, wf, rf, pl_, sl, wbl, sbl, al, be, rrs, pws, ivs,
    xt, xl, mx, sxl, syl, yl, xb, pb, rb, rrb, dsy, dcc,
    src, recv1, buf2, recv2, stat, stat_in,
    in_sem, s1, r1, s2, r2, hs, hr,
):
    me = lax.axis_index("seq")
    my_head = lax.axis_index("head")
    pr = DH // n_seq
    nch = k_in.shape[0] // CH

    pr8 = max(pr, 8)
    own_rows = pl.ds(pl.multiple_of(me * pr // pr8 * pr8, pr8), pr8)
    loads = []
    for at, (source, target) in enumerate(
        ((k_hbm, k_in), (v_hbm, v_in), (q_hbm, q_in), (pg_hbm.at[0, own_rows], pg_in),
         (pc_hbm.at[0, own_rows], pc_in), (cot_hbm, cot_in), (gain_hbm, gain_in),
         (ridge_hbm, ridge_in))
    ):
        copy = pltpu.make_async_copy(source, target, in_sem.at[at])
        copy.start()
        loads.append(copy)

    barrier = pltpu.get_barrier_semaphore()

    def greet_seq(turn, carry):
        pl.semaphore_signal(
            barrier, inc=1, device_id={"seq": lax.rem(me + turn, n_seq)}, device_id_type=MESH
        )
        return carry

    def greet_head(turn, carry):
        pl.semaphore_signal(
            barrier, inc=1, device_id={"head": lax.rem(my_head + turn, n_head)},
            device_id_type=MESH,
        )
        return carry

    lax.fori_loop(1, n_seq, greet_seq, 0)
    lax.fori_loop(1, n_head, greet_head, 0)

    if n_seq == 32:
        offsets = [(x, y, z) for x in range(4) for y in range(4) for z in range(2)]
        offsets = sorted(offsets, key=lambda o: -(hops(o[0]) + hops(o[1])))
        my_x, my_y, my_core = me // 8, lax.rem(me // 2, 4), lax.rem(me, 2)
        others = [
            lax.rem(my_x + x, 4) * 8 + lax.rem(my_y + y, 4) * 2 + lax.rem(my_core + z, 2)
            for x, y, z in offsets
            if (x, y, z) != (0, 0, 0)
        ]
    else:
        others = [lax.rem(me + turn, n_seq) for turn in range(1, n_seq)]
    turns = sorted(range(1, n_head), key=lambda turn: -min(turn, n_head - turn))

    def bytes_wait(ref, count, sem):
        view = ref.at[pl.ds(0, count)]
        pltpu.make_async_copy(view, view, sem).wait()

    def send(x, source, target, send_sem, recv_sem):
        for device in others:
            pltpu.make_async_remote_copy(
                src_ref=source.at[x, device], dst_ref=target.at[x, me],
                send_sem=send_sem.at[x], recv_sem=recv_sem.at[x],
                device_id={"seq": device}, device_id_type=MESH,
            ).start()
        target[x, me] = source[x, me]

    def send_first(x, total):
        src[x] = total.reshape(n_seq, pr, DH)
        send(x, src, recv1, s1, r1)

    def send_second(x, reverse, base):
        bytes_wait(recv1.at[x], n_seq - 1, r1.at[x])
        if base is None:
            total = jnp.zeros((pr, DH), F32)
        elif pr < 8:
            total = base[:pr]
            for part in range(1, 8 // pr):
                total = jnp.where(
                    lax.rem(me, 8 // pr) == part, base[part * pr : (part + 1) * pr], total
                )
        else:
            total = base[...]
        for device in range(n_seq - 1, -1, -1) if reverse else range(n_seq):
            buf2[x, device] = total
            total = total + recv1[x, device]
        send(x, buf2, recv2, s2, r2)

    def finish(x):
        bytes_wait(recv2.at[x], n_seq - 1, r2.at[x])
        return recv2[x].reshape(DH, DH)

    rows = [pl.ds(c * CH, CH) for c in range(nch)]
    keep = (
        lax.broadcasted_iota(jnp.int32, (CH, CH), 0)
        <= lax.broadcasted_iota(jnp.int32, (CH, CH), 1)
    )
    lane = lax.broadcasted_iota(jnp.int32, (8, CH), 1)
    first_row = me * k_in.shape[0]

    loads[0].wait()
    for c in range(nch):
        keys = k_in[rows[c], :]
        ak[c, DH:, :] = left(keys)
        kt[c] = left(keys.T)
    total = mul_cat([(kt[c], ak[c, DH:, :]) for c in range(nch)])
    pl.semaphore_wait(barrier, n_seq - 1 + n_head - 1)
    send_first(0, total)

    loads[1].wait()
    for c in range(nch):
        vl[c] = left(v_in[rows[c], :])
    send_first(1, mul_cat([(kt[c], vl[c]) for c in range(nch)]))

    loads[7].wait()
    damping = [
        ridge_in[0] * (first_row + (c * CH + 1) + lane).astype(F32) for c in range(nch)
    ]
    loads[2].wait()
    for c in range(nch):
        start = q_in[rows[c], :].T
        pf[0, c] = start
        pl_[0, c] = left(start)
        rrs[0, c] = colsum(start * start)
        xt[c] = jnp.zeros_like(start)
    for c in range(nch - 1):
        mg[c] = mul(kt[c], ak[c, DH:, :])
    loads[3].wait()
    send_second(0, False, pg_in)
    for c in range(nch - 1):
        mc[c] = mul(kt[c], vl[c])
    loads[4].wait()
    send_second(1, False, pc_in)
    loads[5].wait()
    loads[6].wait()
    for c in range(nch):
        vtl[c] = left(v_in[rows[c], :].T)
        ct[c] = (cot_in[rows[c], :] * gain_in[...]).T

    gram = finish(0)
    for c in range(nch):
        ak[c, :DH, :] = left(gram)
        if c + 1 < nch:
            gram = gram + mg[c]

    def forward(c):
        for step in range(ITERS):
            both = fold(jnp.dot(ak[c], right(pl_[step, c]), preferred_element_type=F32))
            yield
            inner = left(jnp.where(keep, both[DH:], 0.0))
            sl[step, c] = inner
            yield
            image = both[:DH] + mul(kt[c], inner)
            yield
            search = pf[step, c]
            image = image + scaled(damping[c], search)
            wf[step, c] = image
            curve = 1.0 / colsum(search * image)
            squared = rrs[step, c]
            alpha = squared * curve
            inv = 1.0 / squared
            pws[step, c] = curve
            al[step, c] = alpha
            ivs[step, c] = inv
            yield
            xt[c] = xt[c] + scaled(alpha, search)
            if step + 1 < ITERS:
                before = pf[0, c] if step == 0 else rf[step - 1, c]
                residual = before - scaled(alpha, image)
                rf[step, c] = residual
                squared = colsum(residual * residual)
                beta = squared * inv
                be[step, c] = beta
                rrs[step + 1, c] = squared
                search = residual + scaled(beta, search)
                pf[step + 1, c] = search
                pl_[step + 1, c] = left(search)
            else:
                xl[c] = left(xt[c])
            yield

    interleave([forward(c) for c in range(nch)], (0,1,3,4))

    cross = finish(1)
    for c in range(nch):
        ctl[c] = left(cross.T)
        cl[c] = left(cross)
        if c + 1 < nch:
            cross = cross + mc[c]

    def read_out(c):
        inner = mul(ak[c, DH:, :], xl[c])
        yield
        inner = left(jnp.where(keep, inner, 0.0))
        sxl[c] = inner
        yield
        mixed = mul_cat([(ctl[c], xl[c]), (vtl[c], inner)])
        yield
        mx[c] = mixed
        stat[c : c + 1, :] = colsum(mixed * mixed)[:1]
        stat[nch + c : nch + c + 1, :] = colsum(ct[c] * mixed)[:1]
        yield

    interleave([read_out(c) for c in range(nch)], range(nch))

    for turn in turns:
        pltpu.make_async_remote_copy(
            src_ref=stat, dst_ref=stat_in.at[my_head], send_sem=hs.at[0], recv_sem=hr.at[0],
            device_id={"head": lax.rem(my_head + turn, n_head)}, device_id_type=MESH,
        ).start()
    stat_in[my_head] = stat[...]
    bytes_wait(stat_in, n_head - 1, hr.at[0])
    sums = stat_in[0]
    for device in range(1, n_head):
        sums = sums + stat_in[device]
    inverse = lax.rsqrt(sums[:nch] / features + epsilon)
    pull = inverse * inverse * inverse * (sums[nch:] / features)

    last = ITERS - 1

    def backward(c):
        grad = left(inverse[c : c + 1, :] * ct[c] - mx[c] * pull[c : c + 1, :])
        yl[c] = grad
        inner = mul(vl[c], grad)
        yield
        inner = left(jnp.where(keep, inner, 0.0))
        syl[c] = inner
        yield
        solution_bar = mul_cat([(cl[c], grad), (kt[c], inner)])
        yield
        xb[c] = solution_bar
        search, image = pf[last, c], wf[last, c]
        alpha = al[last, c]
        ratio = colsum(solution_bar * search) * pws[last, c]
        curve_bar = -ratio * alpha
        wbl[last, c] = left(scaled(curve_bar, search))
        halves = sl[last, c]
        sbl[last, c] = left(
            scaled(curve_bar, halves[:, :CH].astype(F32) + halves[:, CH:].astype(F32))
        )
        pb[c] = scaled(alpha, solution_bar) + scaled(2.0 * curve_bar, image)
        rrb[c] = ratio
        yield
        for step in range(last - 1, -1, -1):
            search, search_bar = pf[step, c], pb[c]
            alpha, beta = al[step, c], be[step, c]
            beta_bar = colsum(search_bar * search) * ivs[step, c]
            next_bar = 2.0 * (rrb[c] + beta_bar)
            yield
            residual_bar = search_bar + scaled(next_bar, rf[step, c])
            if step + 1 < last:
                residual_bar = residual_bar + rb[c]
            rb[c] = residual_bar
            image, solution_bar = wf[step, c], xb[c]
            ratio = colsum(solution_bar * search - residual_bar * image) * pws[step, c]
            curve_bar = -ratio * alpha
            rrb[c] = ratio - beta_bar * beta
            image_bar = scaled(curve_bar, search) - scaled(alpha, residual_bar)
            halves = left(image_bar)
            wbl[step, c] = halves
            pb[c] = (
                scaled(beta, search_bar) + scaled(alpha, solution_bar)
                + scaled(curve_bar, image) + scaled(damping[c], image_bar)
            )
            yield
            both = fold(jnp.dot(ak[c], right(halves), preferred_element_type=F32))
            yield
            inner = left(jnp.where(keep, both[DH:], 0.0))
            sbl[step, c] = inner
            yield
            pb[c] = pb[c] + (both[:DH] + mul(kt[c], inner))
            yield

    interleave([backward(c) for c in range(nch)], (0,1,3,4))

    total = jnp.zeros((DH, DH), F32)
    for c in range(nch):
        part = mul_t([(pl_[j, c], wbl[j, c]) for j in range(ITERS)])
        dsy[c] = part
        total = total + part
    send_first(2, total + total.T)
    total = jnp.zeros((DH, DH), F32)
    for c in range(nch):
        part = mul_t([(xl[c], yl[c])])
        dcc[c] = part
        total = total + part
    send_first(3, total)

    for c in range(nch):
        o_normed[rows[c], :] = (mx[c] * inverse[c : c + 1, :]).T * gain_in[...]
        grad = rb[c] + pb[c] + scaled(2.0 * rrb[c], pf[0, c])
        o_gq[rows[c], :] = grad.T

    def key_part(c):
        pairs = [(syl[c], xl[c])]
        for j in range(ITERS):
            pairs.append((sl[j, c], wbl[j, c]))
            pairs.append((sbl[j, c], pl_[j, c]))
        o_gk[rows[c], :] = mul_t(pairs)

    key_part(0)
    key_part(1)
    send_second(2, True, None)
    send_second(3, True, None)
    key_part(2)
    key_part(3)
    later = jnp.zeros((DH, DH), F32)
    for c in range(nch - 1, -1, -1):
        o_gv[rows[c], :] = mul_t([(sxl[c], yl[c])])
        if c + 1 < nch:
            o_gk[rows[c], :] += mul(ak[c, DH:, :], left(later))
        later = later + (dsy[c] + dsy[c].T)

    cross = finish(3)
    for c in range(nch - 1, -1, -1):
        halves = left(cross)
        o_gv[rows[c], :] += mul(ak[c, DH:, :], halves)
        o_gk[rows[c], :] += mul_t([(vl[c], halves)])
        cross = cross + dcc[c]
    halves = left(finish(2))
    for c in range(nch):
        o_gk[rows[c], :] += mul(ak[c, DH:, :], halves)

    bytes_wait(stat_in, n_head - 1, hs.at[0])
    for x in range(4):
        bytes_wait(src.at[x], n_seq - 1, s1.at[x])
        bytes_wait(buf2.at[x], n_seq - 1, s2.at[x])


def hand_over(a, b, c, d, a_out, b_out, c_out, d_out, sem):
    pairs = ((a, a_out), (b, b_out), (c, c_out), (d, d_out))
    copies = [pltpu.make_async_copy(*pair, sem.at[at]) for at, pair in enumerate(pairs)]
    for copy in copies:
        copy.start()
    for copy in copies:
        copy.wait()


def local(n_seq, n_head, queries, keys, values, gain, ridge, prior_gram, prior_cross, cotangent):
    rows, width = queries.shape
    nch = rows // CH
    pr = DH // n_seq
    anyspace = pl.BlockSpec(memory_space=pl.ANY)
    tok = pltpu.VMEM((rows, DH), F32)
    prior = pltpu.VMEM((max(pr, 8), DH), F32)
    per_chunk = pltpu.VMEM((nch, DH, CH), F32)
    halves = pltpu.VMEM((nch, DH, 2 * CH), BF16)
    per_step = pltpu.VMEM((ITERS, nch, DH, CH), F32)
    step_halves = pltpu.VMEM((ITERS, nch, DH, 2 * CH), BF16)
    scal = pltpu.VMEM((ITERS, nch, 8, CH), F32)
    exchange = pltpu.VMEM((4, n_seq, pr, DH), F32)
    scratch = [
        tok, tok, tok, tok, prior, prior, pltpu.VMEM((1, DH), F32), pltpu.SMEM((1,), F32),
        pltpu.VMEM((nch, 2 * DH, 2 * CH), BF16), halves, halves, halves, halves, halves,
        per_chunk, per_chunk, per_chunk, per_chunk,
        per_step, per_step, per_step, step_halves, step_halves, step_halves, step_halves,
        scal, scal, scal, scal, scal,
        per_chunk, halves, per_chunk, halves, halves, halves, per_chunk, per_chunk, per_chunk,
        pltpu.VMEM((nch, 8, CH), F32), per_chunk, per_chunk,
        exchange, exchange, exchange, exchange,
        pltpu.VMEM((2 * nch, CH), F32), pltpu.VMEM((n_head, 2 * nch, CH), F32),
        pltpu.SemaphoreType.DMA((8,)),
        pltpu.SemaphoreType.DMA((4,)), pltpu.SemaphoreType.DMA((4,)),
        pltpu.SemaphoreType.DMA((4,)), pltpu.SemaphoreType.DMA((4,)),
        pltpu.SemaphoreType.DMA((1,)), pltpu.SemaphoreType.DMA((1,)),
    ]
    shape = jax.ShapeDtypeStruct((rows, width), F32)
    held = pltpu.VMEM((rows, width), F32)
    results = pl.pallas_call(
        functools.partial(kernel, n_seq, n_head, float(width * n_head)),
        out_shape=(held, held, held, held),
        in_specs=[pl.BlockSpec(memory_space=pltpu.HBM)] * 8,
        out_specs=[pl.BlockSpec(memory_space=pltpu.VMEM)] * 4,
        scratch_shapes=scratch,
        compiler_params=pltpu.CompilerParams(
            collective_id=0, has_side_effects=True, vmem_limit_bytes=65800000
        ),
    )(
        queries, keys, values, gain.reshape(1, width), ridge,
        prior_gram, prior_cross, cotangent,
    )
    return pl.pallas_call(
        hand_over,
        out_shape=(shape, shape, shape, shape),
        in_specs=[pl.BlockSpec(memory_space=pltpu.VMEM)] * 4,
        out_specs=[pl.BlockSpec(memory_space=pltpu.HBM)] * 4,
        scratch_shapes=[pltpu.SemaphoreType.DMA((4,))],
        compiler_params=pltpu.CompilerParams(vmem_limit_bytes=1024 * 1024),
    )(*results)


def solution(mesh):
    in_specs = (
        P("seq", "head"),
        P("seq", "head"),
        P("seq", "head"),
        P("head"),
        P("head"),
        P("head", None, None),
        P("head", None, None),
        P("seq", "head"),
    )
    out_specs = (P("seq", "head"), P("seq", "head"), P("seq", "head"), P("seq", "head"))
    body = functools.partial(local, mesh.shape["seq"], mesh.shape["head"])
    return jax.shard_map(body, mesh=mesh, in_specs=in_specs, out_specs=out_specs, check_vma=False)
```

```python
import functools

import jax
import jax.numpy as jnp
from jax import lax
from jax.experimental import pallas as pl
from jax.experimental.pallas import tpu as pltpu
from jax.sharding import PartitionSpec as P

DH = 128
ITERS = 8
CH = 128
epsilon = 1e-06

F32 = jnp.float32
BF16 = jnp.bfloat16
MESH = pl.DeviceIdType.MESH


def left(x):
    hi = x.astype(BF16)
    lo = (x - hi.astype(F32)).astype(BF16)
    return jnp.concatenate([hi, lo], axis=1)


def right(halves):
    return jnp.concatenate([halves, halves], axis=0)


def fold(out):
    return out[:, :CH] + out[:, CH:]


def mul(a, b):
    return fold(jnp.dot(a, right(b), preferred_element_type=F32))


def mul_cat(pairs):
    a = jnp.concatenate([pair[0] for pair in pairs], axis=1)
    b = jnp.concatenate([right(pair[1]) for pair in pairs], axis=0)
    return fold(jnp.dot(a, b, preferred_element_type=F32))


def stack(parts):
    his = jnp.concatenate([part[:, :CH] for part in parts], axis=1)
    los = jnp.concatenate([part[:, CH:] for part in parts], axis=1)
    return jnp.concatenate([his, los], axis=0)


def mul_t(pairs):
    out = fold(
        lax.dot_general(
            stack([pair[0] for pair in pairs]), stack([pair[1] for pair in pairs]),
            (((1,), (1,)), ((), ())), preferred_element_type=F32,
        )
    )
    return out[:DH] + out[DH:]


def colsum(x):
    while x.shape[0] > 8:
        half = x.shape[0] // 2
        x = x[:half] + x[half:]
    for shift in (4, 2, 1):
        x = x + pltpu.roll(x, shift, 0)
    return x


def scaled(row, x):
    return (x.reshape(-1, 8, CH) * row).reshape(x.shape)


def interleave(makers, offsets):
    chains = [(maker, late) for maker, late in zip(makers, offsets)]
    turn = 0
    while chains:
        left_over = []
        for chain, late in chains:
            if turn < late or next(chain, True) is None:
                left_over.append((chain, late))
        chains = left_over
        turn += 1


def hops(offset):
    return (0, 1, 2, 1)[offset]


def kernel(
    n_seq, n_head, features,
    q_hbm, k_hbm, v_hbm, gain_hbm, ridge_hbm, pg_hbm, pc_hbm, cot_hbm,
    o_normed, o_gq, o_gk, o_gv,
    q_in, k_in, v_in, cot_in, pg_in, pc_in, gain_in, ridge_in,
    ak, kt, vl, vtl, cl, ctl, mg, mc, qt, ct,
    pf, wf, rf, pl_, sl, wbl, sbl, al, be, rrs, pws, ivs,
    xt, xl, mx, sxl, syl, yl, xb, xm, ml, pb, rb, rrb, dsy, dcc,
    src, recv1, buf2, recv2, stat, stat_in,
    in_sem, s1, r1, s2, r2, hs, hr,
):
    me = lax.axis_index("seq")
    my_head = lax.axis_index("head")
    pr = DH // n_seq
    nch = k_in.shape[0] // CH

    pr8 = max(pr, 8)
    own_rows = pl.ds(pl.multiple_of(me * pr // pr8 * pr8, pr8), pr8)
    loads = []
    for at, (source, target) in enumerate(
        ((k_hbm, k_in), (v_hbm, v_in), (q_hbm, q_in), (pg_hbm.at[0, own_rows], pg_in),
         (pc_hbm.at[0, own_rows], pc_in), (cot_hbm, cot_in), (gain_hbm, gain_in),
         (ridge_hbm, ridge_in))
    ):
        copy = pltpu.make_async_copy(source, target, in_sem.at[at])
        copy.start()
        loads.append(copy)

    barrier = pltpu.get_barrier_semaphore()

    if n_seq == 32:
        offsets = [(x, y, z) for x in range(4) for y in range(4) for z in range(2)]
        offsets = sorted(offsets, key=lambda o: -(hops(o[0]) + hops(o[1])))
        my_x, my_y, my_core = me // 8, lax.rem(me // 2, 4), lax.rem(me, 2)
        others = [
            lax.rem(my_x + x, 4) * 8 + lax.rem(my_y + y, 4) * 2 + lax.rem(my_core + z, 2)
            for x, y, z in offsets
            if (x, y, z) != (0, 0, 0)
        ]
    else:
        others = [lax.rem(me + turn, n_seq) for turn in range(1, n_seq)]
    turns = sorted(range(1, n_head), key=lambda turn: -min(turn, n_head - turn))
    for device in others:
        pl.semaphore_signal(barrier, inc=1, device_id={"seq": device}, device_id_type=MESH)
    for turn in turns:
        pl.semaphore_signal(
            barrier, inc=1, device_id={"head": lax.rem(my_head + turn, n_head)},
            device_id_type=MESH,
        )

    def bytes_wait(ref, count, sem):
        view = ref.at[pl.ds(0, count)]
        pltpu.make_async_copy(view, view, sem).wait()

    def send(x, source, target, send_sem, recv_sem):
        for device in others:
            pltpu.make_async_remote_copy(
                src_ref=source.at[x, device], dst_ref=target.at[x, me],
                send_sem=send_sem.at[x], recv_sem=recv_sem.at[x],
                device_id={"seq": device}, device_id_type=MESH,
            ).start()
        target[x, me] = source[x, me]

    def send_first(x, total):
        src[x] = total.reshape(n_seq, pr, DH)
        send(x, src, recv1, s1, r1)

    def send_second(x, reverse, base):
        bytes_wait(recv1.at[x], n_seq - 1, r1.at[x])
        if base is None:
            total = jnp.zeros((pr, DH), F32)
        elif pr < 8:
            total = base[:pr]
            for part in range(1, 8 // pr):
                total = jnp.where(
                    lax.rem(me, 8 // pr) == part, base[part * pr : (part + 1) * pr], total
                )
        else:
            total = base[...]
        for device in range(n_seq - 1, -1, -1) if reverse else range(n_seq):
            buf2[x, device] = total
            total = total + recv1[x, device]
        send(x, buf2, recv2, s2, r2)

    def finish(x):
        bytes_wait(recv2.at[x], n_seq - 1, r2.at[x])
        return recv2[x].reshape(DH, DH)

    rows = [pl.ds(c * CH, CH) for c in range(nch)]
    keep = (
        lax.broadcasted_iota(jnp.int32, (CH, CH), 0)
        <= lax.broadcasted_iota(jnp.int32, (CH, CH), 1)
    )
    lane = lax.broadcasted_iota(jnp.int32, (8, CH), 1)
    first_row = me * k_in.shape[0]

    loads[0].wait()
    for c in range(nch):
        keys = k_in[rows[c], :]
        ak[c, DH:, :] = left(keys)
        kt[c] = left(keys.T)
    total = mul_cat([(kt[c], ak[c, DH:, :]) for c in range(nch)])
    pl.semaphore_wait(barrier, n_seq - 1 + n_head - 1)
    send_first(0, total)

    loads[1].wait()
    for c in range(nch):
        vl[c] = left(v_in[rows[c], :])
    send_first(1, mul_cat([(kt[c], vl[c]) for c in range(nch)]))

    loads[7].wait()
    damping = [
        ridge_in[0] * (first_row + (c * CH + 1) + lane).astype(F32) for c in range(nch)
    ]
    loads[2].wait()
    for c in range(nch):
        start = q_in[rows[c], :].T
        pf[0, c] = start
        pl_[0, c] = left(start)
        rrs[0, c] = colsum(start * start)
        xt[c] = jnp.zeros_like(start)
        sl[0, c] = left(jnp.where(keep, mul(ak[c, DH:, :], pl_[0, c]), 0.0))
    for c in range(nch - 1):
        mg[c] = mul(kt[c], ak[c, DH:, :])
    loads[3].wait()
    send_second(0, False, pg_in)
    for c in range(nch - 1):
        mc[c] = mul(kt[c], vl[c])
    loads[4].wait()
    send_second(1, False, pc_in)
    loads[5].wait()
    loads[6].wait()
    for c in range(nch):
        vtl[c] = left(v_in[rows[c], :].T)
        ct[c] = (cot_in[rows[c], :] * gain_in[...]).T

    gram = finish(0)
    for c in range(nch):
        ak[c, :DH, :] = left(gram)
        if c + 1 < nch:
            gram = gram + mg[c]

    def forward(c):
        for step in range(ITERS):
            halves = pl_[step, c]
            if step == 0:
                inner = sl[0, c]
            else:
                inner = mul(ak[c, DH:, :], halves)
                yield
                inner = left(jnp.where(keep, inner, 0.0))
                sl[step, c] = inner
                yield
            image = mul_cat([(ak[c, :DH, :], halves), (kt[c], inner)])
            yield
            search = pf[step, c]
            image = image + scaled(damping[c], search)
            wf[step, c] = image
            curve = 1.0 / colsum(search * image)
            squared = rrs[step, c]
            alpha = squared * curve
            inv = 1.0 / squared
            pws[step, c] = curve
            al[step, c] = alpha
            ivs[step, c] = inv
            yield
            xt[c] = xt[c] + scaled(alpha, search)
            if step + 1 < ITERS:
                before = pf[0, c] if step == 0 else rf[step - 1, c]
                residual = before - scaled(alpha, image)
                rf[step, c] = residual
                squared = colsum(residual * residual)
                beta = squared * inv
                be[step, c] = beta
                rrs[step + 1, c] = squared
                search = residual + scaled(beta, search)
                pf[step + 1, c] = search
                pl_[step + 1, c] = left(search)
            else:
                xl[c] = left(xt[c])
            yield

    def cross_states():
        cross = finish(1)
        for c in range(nch):
            yield
            ctl[c] = left(cross.T)
            cl[c] = left(cross)
            if c + 1 < nch:
                cross = cross + mc[c]
            yield
            grad = left(ct[c])
            inner = left(jnp.where(keep, mul(vl[c], grad), 0.0))
            yield
            xb[c] = mul_cat([(cl[c], grad), (kt[c], inner)])
            yield

    interleave([forward(c) for c in range(nch)] + [cross_states()], (0, 0, 0, 0, 12))

    def read_out(c):
        inner = mul(ak[c, DH:, :], xl[c])
        yield
        inner = left(jnp.where(keep, inner, 0.0))
        sxl[c] = inner
        yield
        mixed = mul_cat([(ctl[c], xl[c]), (vtl[c], inner)])
        yield
        mx[c] = mixed
        stat[c : c + 1, :] = colsum(mixed * mixed)[:1]
        stat[nch + c : nch + c + 1, :] = colsum(ct[c] * mixed)[:1]
        yield

    interleave([read_out(c) for c in range(nch)], range(nch))

    for turn in turns:
        pltpu.make_async_remote_copy(
            src_ref=stat, dst_ref=stat_in.at[my_head], send_sem=hs.at[0], recv_sem=hr.at[0],
            device_id={"head": lax.rem(my_head + turn, n_head)}, device_id_type=MESH,
        ).start()
    stat_in[my_head] = stat[...]
    for c in range(nch):
        ml[c] = left(mx[c])
        inner = left(jnp.where(keep, mul(vl[c], ml[c]), 0.0))
        xm[c] = mul_cat([(cl[c], ml[c]), (kt[c], inner)])
    bytes_wait(stat_in, n_head - 1, hr.at[0])
    sums = stat_in[0]
    for device in range(1, n_head):
        sums = sums + stat_in[device]
    inverse = lax.rsqrt(sums[:nch] / features + epsilon)
    pull = inverse * inverse * inverse * (sums[nch:] / features)

    last = ITERS - 1

    def push_back(c, step, halves):
        inner = mul(ak[c, DH:, :], halves)
        yield
        inner = left(jnp.where(keep, inner, 0.0))
        sbl[step, c] = inner
        yield
        pb[c] = pb[c] + mul_cat([(ak[c, :DH, :], halves), (kt[c], inner)])

    def backward(c):
        keep_part = jnp.broadcast_to(inverse[c : c + 1, :], (8, CH))
        norm_part = jnp.broadcast_to(pull[c : c + 1, :], (8, CH))
        solution_bar = scaled(keep_part, xb[c]) - scaled(norm_part, xm[c])
        xb[c] = solution_bar
        search, image = pf[last, c], wf[last, c]
        alpha = al[last, c]
        ratio = colsum(solution_bar * search) * pws[last, c]
        curve_bar = -ratio * alpha
        wbl[last, c] = left(scaled(curve_bar, search))
        halves = sl[last, c]
        sbl[last, c] = left(
            scaled(curve_bar, halves[:, :CH].astype(F32) + halves[:, CH:].astype(F32))
        )
        pb[c] = scaled(alpha, solution_bar) + scaled(2.0 * curve_bar, image)
        rrb[c] = ratio
        yield
        for step in range(last - 1, -1, -1):
            search, search_bar = pf[step, c], pb[c]
            alpha, beta = al[step, c], be[step, c]
            beta_bar = colsum(search_bar * search) * ivs[step, c]
            next_bar = 2.0 * (rrb[c] + beta_bar)
            yield
            residual_bar = search_bar + scaled(next_bar, rf[step, c])
            if step + 1 < last:
                residual_bar = residual_bar + rb[c]
            rb[c] = residual_bar
            image, solution_bar = wf[step, c], xb[c]
            ratio = colsum(solution_bar * search - residual_bar * image) * pws[step, c]
            curve_bar = -ratio * alpha
            rrb[c] = ratio - beta_bar * beta
            image_bar = scaled(curve_bar, search) - scaled(alpha, residual_bar)
            halves = left(image_bar)
            wbl[step, c] = halves
            pb[c] = (
                scaled(beta, search_bar) + scaled(alpha, solution_bar)
                + scaled(curve_bar, image) + scaled(damping[c], image_bar)
            )
            yield
            if step % 2 == 0:
                part = mul_t([(pl_[j, c], wbl[j, c]) for j in (step + 1, step)])
                dsy[c] = part if step + 2 > last else dsy[c] + part
            if step > 0:
                yield from push_back(c, step, halves)
                yield

    def cross_back():
        total = jnp.zeros((DH, DH), F32)
        for c in range(nch):
            yl[c] = left(inverse[c : c + 1, :] * ct[c] - mx[c] * pull[c : c + 1, :])
            part = mul_t([(xl[c], yl[c])])
            dcc[c] = part
            total = total + part
            yield
        send_first(3, total)
        yield

    interleave([backward(c) for c in range(nch)] + [cross_back()], (0, 0, 0, 0, 2))

    total = dsy[0]
    for c in range(1, nch):
        total = total + dsy[c]
    send_first(2, total + total.T)
    interleave([push_back(c, 0, wbl[0, c]) for c in range(nch)], (0, 0, 0, 0))
    for c in range(nch):
        syl[c] = left(jnp.where(keep, mul(vl[c], yl[c]), 0.0))
        o_normed[rows[c], :] = (mx[c] * inverse[c : c + 1, :]).T * gain_in[...]
        grad = rb[c] + pb[c] + scaled(2.0 * rrb[c], pf[0, c])
        o_gq[rows[c], :] = grad.T

    def key_part(c):
        pairs = [(syl[c], xl[c])]
        for j in range(ITERS):
            pairs.append((sl[j, c], wbl[j, c]))
            pairs.append((sbl[j, c], pl_[j, c]))
        o_gk[rows[c], :] = mul_t(pairs)

    send_second(3, True, None)
    key_part(0)
    send_second(2, True, None)
    key_part(1)
    key_part(2)
    key_part(3)
    later = jnp.zeros((DH, DH), F32)
    for c in range(nch - 1, -1, -1):
        o_gv[rows[c], :] = mul_t([(sxl[c], yl[c])])
        if c + 1 < nch:
            o_gk[rows[c], :] += mul(ak[c, DH:, :], left(later))
        later = later + (dsy[c] + dsy[c].T)

    cross = finish(3)
    for c in range(nch - 1, -1, -1):
        halves = left(cross)
        o_gv[rows[c], :] += mul(ak[c, DH:, :], halves)
        o_gk[rows[c], :] += mul_t([(vl[c], halves)])
        cross = cross + dcc[c]
    halves = left(finish(2))
    for c in range(nch):
        o_gk[rows[c], :] += mul(ak[c, DH:, :], halves)

    bytes_wait(stat_in, n_head - 1, hs.at[0])
    for x in range(4):
        bytes_wait(src.at[x], n_seq - 1, s1.at[x])
        bytes_wait(buf2.at[x], n_seq - 1, s2.at[x])


def hand_over(a, b, c, d, a_out, b_out, c_out, d_out, sem):
    pairs = ((a, a_out), (b, b_out), (c, c_out), (d, d_out))
    copies = [pltpu.make_async_copy(*pair, sem.at[at]) for at, pair in enumerate(pairs)]
    for copy in copies:
        copy.start()
    for copy in copies:
        copy.wait()


def local(n_seq, n_head, queries, keys, values, gain, ridge, prior_gram, prior_cross, cotangent):
    rows, width = queries.shape
    nch = rows // CH
    pr = DH // n_seq
    anyspace = pl.BlockSpec(memory_space=pl.ANY)
    tok = pltpu.VMEM((rows, DH), F32)
    prior = pltpu.VMEM((max(pr, 8), DH), F32)
    per_chunk = pltpu.VMEM((nch, DH, CH), F32)
    halves = pltpu.VMEM((nch, DH, 2 * CH), BF16)
    per_step = pltpu.VMEM((ITERS, nch, DH, CH), F32)
    step_halves = pltpu.VMEM((ITERS, nch, DH, 2 * CH), BF16)
    scal = pltpu.VMEM((ITERS, nch, 8, CH), F32)
    exchange = pltpu.VMEM((4, n_seq, pr, DH), F32)
    scratch = [
        tok, tok, tok, tok, prior, prior, pltpu.VMEM((1, DH), F32), pltpu.SMEM((1,), F32),
        pltpu.VMEM((nch, 2 * DH, 2 * CH), BF16), halves, halves, halves, halves, halves,
        per_chunk, per_chunk, per_chunk, per_chunk,
        per_step, per_step, per_step, step_halves, step_halves, step_halves, step_halves,
        scal, scal, scal, scal, scal,
        per_chunk, halves, per_chunk, halves, halves, halves, per_chunk, per_chunk, halves, per_chunk, per_chunk,
        pltpu.VMEM((nch, 8, CH), F32), per_chunk, per_chunk,
        exchange, exchange, exchange, exchange,
        pltpu.VMEM((2 * nch, CH), F32), pltpu.VMEM((n_head, 2 * nch, CH), F32),
        pltpu.SemaphoreType.DMA((8,)),
        pltpu.SemaphoreType.DMA((4,)), pltpu.SemaphoreType.DMA((4,)),
        pltpu.SemaphoreType.DMA((4,)), pltpu.SemaphoreType.DMA((4,)),
        pltpu.SemaphoreType.DMA((1,)), pltpu.SemaphoreType.DMA((1,)),
    ]
    shape = jax.ShapeDtypeStruct((rows, width), F32)
    held = pltpu.VMEM((rows, width), F32)
    results = pl.pallas_call(
        functools.partial(kernel, n_seq, n_head, float(width * n_head)),
        out_shape=(held, held, held, held),
        in_specs=[pl.BlockSpec(memory_space=pltpu.HBM)] * 8,
        out_specs=[pl.BlockSpec(memory_space=pltpu.VMEM)] * 4,
        scratch_shapes=scratch,
        compiler_params=pltpu.CompilerParams(
            collective_id=0, has_side_effects=True, vmem_limit_bytes=65800000
        ),
    )(
        queries, keys, values, gain.reshape(1, width), ridge,
        prior_gram, prior_cross, cotangent,
    )
    return pl.pallas_call(
        hand_over,
        out_shape=(shape, shape, shape, shape),
        in_specs=[pl.BlockSpec(memory_space=pltpu.VMEM)] * 4,
        out_specs=[pl.BlockSpec(memory_space=pltpu.HBM)] * 4,
        scratch_shapes=[pltpu.SemaphoreType.DMA((4,))],
        compiler_params=pltpu.CompilerParams(vmem_limit_bytes=1024 * 1024),
    )(*results)


def solution(mesh):
    in_specs = (
        P("seq", "head"),
        P("seq", "head"),
        P("seq", "head"),
        P("head"),
        P("head"),
        P("head", None, None),
        P("head", None, None),
        P("seq", "head"),
    )
    out_specs = (P("seq", "head"), P("seq", "head"), P("seq", "head"), P("seq", "head"))
    body = functools.partial(local, mesh.shape["seq"], mesh.shape["head"])
    return jax.shard_map(body, mesh=mesh, in_specs=in_specs, out_specs=out_specs, check_vma=False)
```

```python
import functools

import jax
import jax.numpy as jnp
from jax import lax
from jax.experimental import pallas as pl
from jax.experimental.pallas import tpu as pltpu
from jax.sharding import PartitionSpec as P

DH = 128
ITERS = 8
CH = 128
epsilon = 1e-06

F32 = jnp.float32
BF16 = jnp.bfloat16
MESH = pl.DeviceIdType.MESH


def left(x):
    hi = x.astype(BF16)
    lo = (x - hi.astype(F32)).astype(BF16)
    return jnp.concatenate([hi, lo], axis=1)


def right(halves):
    return jnp.concatenate([halves, halves], axis=0)


def fold(out):
    return out[:, :CH] + out[:, CH:]


def mul(a, b):
    return fold(jnp.dot(a, right(b), preferred_element_type=F32))


def mul_cat(pairs):
    a = jnp.concatenate([pair[0] for pair in pairs], axis=1)
    b = jnp.concatenate([right(pair[1]) for pair in pairs], axis=0)
    return fold(jnp.dot(a, b, preferred_element_type=F32))


def stack(parts):
    his = jnp.concatenate([part[:, :CH] for part in parts], axis=1)
    los = jnp.concatenate([part[:, CH:] for part in parts], axis=1)
    return jnp.concatenate([his, los], axis=0)


def mul_t(pairs):
    out = fold(
        lax.dot_general(
            stack([pair[0] for pair in pairs]), stack([pair[1] for pair in pairs]),
            (((1,), (1,)), ((), ())), preferred_element_type=F32,
        )
    )
    return out[:DH] + out[DH:]


def colsum(x):
    while x.shape[0] > 8:
        half = x.shape[0] // 2
        x = x[:half] + x[half:]
    for shift in (4, 2, 1):
        x = x + pltpu.roll(x, shift, 0)
    return x


def scaled(row, x):
    return (x.reshape(-1, 8, CH) * row).reshape(x.shape)


def interleave(makers, offsets):
    chains = [(maker, late) for maker, late in zip(makers, offsets)]
    turn = 0
    while chains:
        left_over = []
        for chain, late in chains:
            if turn < late or next(chain, True) is None:
                left_over.append((chain, late))
        chains = left_over
        turn += 1


def hops(offset):
    return (0, 1, 2, 1)[offset]


def kernel(
    n_seq, n_head, features,
    q_hbm, k_hbm, v_hbm, gain_hbm, ridge_hbm, pg_hbm, pc_hbm, cot_hbm,
    o_normed, o_gq, o_gk, o_gv,
    q_in, k_in, v_in, cot_in, pg_in, pc_in, gain_in, ridge_in,
    ak, kt, vl, vtl, cl, ctl, mg, mc, qt, ct,
    pf, wf, rf, pl_, sl, wbl, sbl, al, be, rrs, pws, ivs,
    xt, xl, mx, sxl, syl, yl, xb, xm, ml, pb, rb, rrb, dsy, dcc,
    src, recv1, buf2, recv2, stat, stat_in,
    in_sem, s1, r1, s2, r2, hs, hr,
):
    me = lax.axis_index("seq")
    my_head = lax.axis_index("head")
    pr = DH // n_seq
    nch = k_in.shape[0] // CH

    pr8 = max(pr, 8)
    own_rows = pl.ds(pl.multiple_of(me * pr // pr8 * pr8, pr8), pr8)
    loads = []
    for at, (source, target) in enumerate(
        ((k_hbm, k_in), (v_hbm, v_in), (q_hbm, q_in), (pg_hbm.at[0, own_rows], pg_in),
         (pc_hbm.at[0, own_rows], pc_in), (cot_hbm, cot_in), (gain_hbm, gain_in),
         (ridge_hbm, ridge_in))
    ):
        copy = pltpu.make_async_copy(source, target, in_sem.at[at])
        copy.start()
        loads.append(copy)

    barrier = pltpu.get_barrier_semaphore()

    if n_seq == 32:
        offsets = [(x, y, z) for x in range(4) for y in range(4) for z in range(2)]
        offsets = sorted(offsets, key=lambda o: -(hops(o[0]) + hops(o[1])))
        my_x, my_y, my_core = me // 8, lax.rem(me // 2, 4), lax.rem(me, 2)
        others = [
            lax.rem(my_x + x, 4) * 8 + lax.rem(my_y + y, 4) * 2 + lax.rem(my_core + z, 2)
            for x, y, z in offsets
            if (x, y, z) != (0, 0, 0)
        ]
    else:
        others = [lax.rem(me + turn, n_seq) for turn in range(1, n_seq)]
    turns = sorted(range(1, n_head), key=lambda turn: -min(turn, n_head - turn))
    for device in others:
        pl.semaphore_signal(barrier, inc=1, device_id={"seq": device}, device_id_type=MESH)
    for turn in turns:
        pl.semaphore_signal(
            barrier, inc=1, device_id={"head": lax.rem(my_head + turn, n_head)},
            device_id_type=MESH,
        )

    def bytes_wait(ref, count, sem):
        view = ref.at[pl.ds(0, count)]
        pltpu.make_async_copy(view, view, sem).wait()

    def send(x, source, target, send_sem, recv_sem):
        for device in others:
            pltpu.make_async_remote_copy(
                src_ref=source.at[x, device], dst_ref=target.at[x, me],
                send_sem=send_sem.at[x], recv_sem=recv_sem.at[x],
                device_id={"seq": device}, device_id_type=MESH,
            ).start()
        target[x, me] = source[x, me]

    def send_first(x, total):
        src[x] = total.reshape(n_seq, pr, DH)
        send(x, src, recv1, s1, r1)

    def send_second(x, reverse, base):
        bytes_wait(recv1.at[x], n_seq - 1, r1.at[x])
        if base is None:
            total = jnp.zeros((pr, DH), F32)
        elif pr < 8:
            total = base[:pr]
            for part in range(1, 8 // pr):
                total = jnp.where(
                    lax.rem(me, 8 // pr) == part, base[part * pr : (part + 1) * pr], total
                )
        else:
            total = base[...]
        for device in range(n_seq - 1, -1, -1) if reverse else range(n_seq):
            buf2[x, device] = total
            total = total + recv1[x, device]
        send(x, buf2, recv2, s2, r2)

    def finish(x):
        bytes_wait(recv2.at[x], n_seq - 1, r2.at[x])
        return recv2[x].reshape(DH, DH)

    rows = [pl.ds(c * CH, CH) for c in range(nch)]
    keep = (
        lax.broadcasted_iota(jnp.int32, (CH, CH), 0)
        <= lax.broadcasted_iota(jnp.int32, (CH, CH), 1)
    )
    lane = lax.broadcasted_iota(jnp.int32, (8, CH), 1)
    first_row = me * k_in.shape[0]

    loads[0].wait()
    for c in range(nch):
        keys = k_in[rows[c], :]
        ak[c, DH:, :] = left(keys)
        kt[c] = left(keys.T)
    total = mul_cat([(kt[c], ak[c, DH:, :]) for c in range(nch)])
    pl.semaphore_wait(barrier, n_seq - 1 + n_head - 1)
    send_first(0, total)

    loads[1].wait()
    for c in range(nch):
        vl[c] = left(v_in[rows[c], :])
    send_first(1, mul_cat([(kt[c], vl[c]) for c in range(nch)]))

    loads[7].wait()
    damping = [
        ridge_in[0] * (first_row + (c * CH + 1) + lane).astype(F32) for c in range(nch)
    ]
    loads[2].wait()
    for c in range(nch):
        start = q_in[rows[c], :].T
        pf[0, c] = start
        pl_[0, c] = left(start)
        rrs[0, c] = colsum(start * start)
        xt[c] = jnp.zeros_like(start)
        sl[0, c] = left(jnp.where(keep, mul(ak[c, DH:, :], pl_[0, c]), 0.0))
    for c in range(nch - 1):
        mg[c] = mul(kt[c], ak[c, DH:, :])
    loads[3].wait()
    send_second(0, False, pg_in)
    for c in range(nch - 1):
        mc[c] = mul(kt[c], vl[c])
    loads[4].wait()
    send_second(1, False, pc_in)
    loads[5].wait()
    loads[6].wait()
    for c in range(nch):
        vtl[c] = left(v_in[rows[c], :].T)
        ct[c] = (cot_in[rows[c], :] * gain_in[...]).T

    gram = finish(0)
    for c in range(nch):
        ak[c, :DH, :] = left(gram)
        if c + 1 < nch:
            gram = gram + mg[c]

    def forward(c):
        for step in range(ITERS):
            halves = pl_[step, c]
            if step == 0:
                inner = sl[0, c]
            else:
                inner = mul(ak[c, DH:, :], halves)
                yield
                inner = left(jnp.where(keep, inner, 0.0))
                sl[step, c] = inner
                yield
            image = mul_cat([(ak[c, :DH, :], halves), (kt[c], inner)])
            yield
            search = pf[step, c]
            image = image + scaled(damping[c], search)
            wf[step, c] = image
            curve = 1.0 / colsum(search * image)
            squared = rrs[step, c]
            alpha = squared * curve
            inv = 1.0 / squared
            pws[step, c] = curve
            al[step, c] = alpha
            ivs[step, c] = inv
            yield
            xt[c] = xt[c] + scaled(alpha, search)
            if step + 1 < ITERS:
                before = pf[0, c] if step == 0 else rf[step - 1, c]
                residual = before - scaled(alpha, image)
                rf[step, c] = residual
                squared = colsum(residual * residual)
                beta = squared * inv
                be[step, c] = beta
                rrs[step + 1, c] = squared
                search = residual + scaled(beta, search)
                pf[step + 1, c] = search
                pl_[step + 1, c] = left(search)
            else:
                xl[c] = left(xt[c])
            yield

    def cross_states():
        cross = finish(1)
        for c in range(nch):
            yield
            ctl[c] = left(cross.T)
            cl[c] = left(cross)
            if c + 1 < nch:
                cross = cross + mc[c]
            yield
            grad = left(ct[c])
            inner = left(jnp.where(keep, mul(vl[c], grad), 0.0))
            yield
            xb[c] = mul_cat([(cl[c], grad), (kt[c], inner)])
            yield

    interleave([forward(c) for c in range(nch)] + [cross_states()], (0, 0, 0, 0, 12))

    def read_out(c):
        inner = mul(ak[c, DH:, :], xl[c])
        yield
        inner = left(jnp.where(keep, inner, 0.0))
        sxl[c] = inner
        yield
        mixed = mul_cat([(ctl[c], xl[c]), (vtl[c], inner)])
        yield
        mx[c] = mixed
        stat[c : c + 1, :] = colsum(mixed * mixed)[:1]
        stat[nch + c : nch + c + 1, :] = colsum(ct[c] * mixed)[:1]
        yield

    interleave([read_out(c) for c in range(nch)], range(nch))

    for turn in turns:
        pltpu.make_async_remote_copy(
            src_ref=stat, dst_ref=stat_in.at[my_head], send_sem=hs.at[0], recv_sem=hr.at[0],
            device_id={"head": lax.rem(my_head + turn, n_head)}, device_id_type=MESH,
        ).start()
    stat_in[my_head] = stat[...]
    for c in range(nch):
        ml[c] = left(mx[c])
        inner = left(jnp.where(keep, mul(vl[c], ml[c]), 0.0))
        xm[c] = mul_cat([(cl[c], ml[c]), (kt[c], inner)])
    bytes_wait(stat_in, n_head - 1, hr.at[0])
    sums = stat_in[0]
    for device in range(1, n_head):
        sums = sums + stat_in[device]
    inverse = lax.rsqrt(sums[:nch] / features + epsilon)
    pull = inverse * inverse * inverse * (sums[nch:] / features)

    last = ITERS - 1

    def push_back(c, step, halves):
        inner = mul(ak[c, DH:, :], halves)
        yield
        inner = left(jnp.where(keep, inner, 0.0))
        sbl[step, c] = inner
        yield
        pb[c] = pb[c] + mul_cat([(ak[c, :DH, :], halves), (kt[c], inner)])

    def backward(c):
        keep_part = jnp.broadcast_to(inverse[c : c + 1, :], (8, CH))
        norm_part = jnp.broadcast_to(pull[c : c + 1, :], (8, CH))
        solution_bar = scaled(keep_part, xb[c]) - scaled(norm_part, xm[c])
        xb[c] = solution_bar
        search, image = pf[last, c], wf[last, c]
        alpha = al[last, c]
        ratio = colsum(solution_bar * search) * pws[last, c]
        curve_bar = -ratio * alpha
        wbl[last, c] = left(scaled(curve_bar, search))
        halves = sl[last, c]
        sbl[last, c] = left(
            scaled(curve_bar, halves[:, :CH].astype(F32) + halves[:, CH:].astype(F32))
        )
        pb[c] = scaled(alpha, solution_bar) + scaled(2.0 * curve_bar, image)
        rrb[c] = ratio
        yield
        for step in range(last - 1, -1, -1):
            search, search_bar = pf[step, c], pb[c]
            alpha, beta = al[step, c], be[step, c]
            beta_bar = colsum(search_bar * search) * ivs[step, c]
            next_bar = 2.0 * (rrb[c] + beta_bar)
            yield
            residual_bar = search_bar + scaled(next_bar, rf[step, c])
            if step + 1 < last:
                residual_bar = residual_bar + rb[c]
            rb[c] = residual_bar
            image, solution_bar = wf[step, c], xb[c]
            ratio = colsum(solution_bar * search - residual_bar * image) * pws[step, c]
            curve_bar = -ratio * alpha
            rrb[c] = ratio - beta_bar * beta
            image_bar = scaled(curve_bar, search) - scaled(alpha, residual_bar)
            halves = left(image_bar)
            wbl[step, c] = halves
            pb[c] = (
                scaled(beta, search_bar) + scaled(alpha, solution_bar)
                + scaled(curve_bar, image) + scaled(damping[c], image_bar)
            )
            yield
            if step % 2 == 0:
                part = mul_t([(pl_[j, c], wbl[j, c]) for j in (step + 1, step)])
                dsy[c] = part if step + 2 > last else dsy[c] + part
            if step > 0:
                yield from push_back(c, step, halves)
                yield

    def cross_back():
        total = jnp.zeros((DH, DH), F32)
        for c in range(nch):
            yl[c] = left(inverse[c : c + 1, :] * ct[c] - mx[c] * pull[c : c + 1, :])
            part = mul_t([(xl[c], yl[c])])
            dcc[c] = part
            total = total + part
            yield
        send_first(3, total)
        yield

    interleave([backward(c) for c in range(nch)] + [cross_back()], (0, 0, 0, 0, 2))

    total = dsy[0]
    for c in range(1, nch):
        total = total + dsy[c]
    send_first(2, total + total.T)
    interleave([push_back(c, 0, wbl[0, c]) for c in range(nch)], (0, 0, 0, 0))
    for c in range(nch):
        syl[c] = left(jnp.where(keep, mul(vl[c], yl[c]), 0.0))
        o_normed[rows[c], :] = (mx[c] * inverse[c : c + 1, :]).T * gain_in[...]
        grad = rb[c] + pb[c] + scaled(2.0 * rrb[c], pf[0, c])
        o_gq[rows[c], :] = grad.T

    def key_part(c):
        pairs = [(syl[c], xl[c])]
        for j in range(ITERS):
            pairs.append((sl[j, c], wbl[j, c]))
            pairs.append((sbl[j, c], pl_[j, c]))
        o_gk[rows[c], :] = mul_t(pairs)

    send_second(3, True, None)
    key_part(0)
    send_second(2, True, None)
    key_part(1)
    key_part(2)
    key_part(3)
    later = jnp.zeros((DH, DH), F32)
    for c in range(nch - 1, -1, -1):
        o_gv[rows[c], :] = mul_t([(sxl[c], yl[c])])
        if c + 1 < nch:
            o_gk[rows[c], :] += mul(ak[c, DH:, :], left(later))
        later = later + (dsy[c] + dsy[c].T)

    cross = finish(3)
    for c in range(nch - 1, -1, -1):
        halves = left(cross)
        o_gv[rows[c], :] += mul(ak[c, DH:, :], halves)
        o_gk[rows[c], :] += mul_t([(vl[c], halves)])
        cross = cross + dcc[c]
    halves = left(finish(2))
    o_gk[...] += mul(jnp.concatenate([ak[c, DH:, :] for c in range(nch)], axis=0), halves)

    bytes_wait(stat_in, n_head - 1, hs.at[0])
    for x in range(4):
        bytes_wait(src.at[x], n_seq - 1, s1.at[x])
        bytes_wait(buf2.at[x], n_seq - 1, s2.at[x])


def hand_over(a, b, c, d, a_out, b_out, c_out, d_out, sem):
    pairs = ((a, a_out), (b, b_out), (c, c_out), (d, d_out))
    copies = [pltpu.make_async_copy(*pair, sem.at[at]) for at, pair in enumerate(pairs)]
    for copy in copies:
        copy.start()
    for copy in copies:
        copy.wait()


def local(n_seq, n_head, queries, keys, values, gain, ridge, prior_gram, prior_cross, cotangent):
    rows, width = queries.shape
    nch = rows // CH
    pr = DH // n_seq
    anyspace = pl.BlockSpec(memory_space=pl.ANY)
    tok = pltpu.VMEM((rows, DH), F32)
    prior = pltpu.VMEM((max(pr, 8), DH), F32)
    per_chunk = pltpu.VMEM((nch, DH, CH), F32)
    halves = pltpu.VMEM((nch, DH, 2 * CH), BF16)
    per_step = pltpu.VMEM((ITERS, nch, DH, CH), F32)
    step_halves = pltpu.VMEM((ITERS, nch, DH, 2 * CH), BF16)
    scal = pltpu.VMEM((ITERS, nch, 8, CH), F32)
    exchange = pltpu.VMEM((4, n_seq, pr, DH), F32)
    scratch = [
        tok, tok, tok, tok, prior, prior, pltpu.VMEM((1, DH), F32), pltpu.SMEM((1,), F32),
        pltpu.VMEM((nch, 2 * DH, 2 * CH), BF16), halves, halves, halves, halves, halves,
        per_chunk, per_chunk, per_chunk, per_chunk,
        per_step, per_step, per_step, step_halves, step_halves, step_halves, step_halves,
        scal, scal, scal, scal, scal,
        per_chunk, halves, per_chunk, halves, halves, halves, per_chunk, per_chunk, halves, per_chunk, per_chunk,
        pltpu.VMEM((nch, 8, CH), F32), per_chunk, per_chunk,
        exchange, exchange, exchange, exchange,
        pltpu.VMEM((2 * nch, CH), F32), pltpu.VMEM((n_head, 2 * nch, CH), F32),
        pltpu.SemaphoreType.DMA((8,)),
        pltpu.SemaphoreType.DMA((4,)), pltpu.SemaphoreType.DMA((4,)),
        pltpu.SemaphoreType.DMA((4,)), pltpu.SemaphoreType.DMA((4,)),
        pltpu.SemaphoreType.DMA((1,)), pltpu.SemaphoreType.DMA((1,)),
    ]
    shape = jax.ShapeDtypeStruct((rows, width), F32)
    held = pltpu.VMEM((rows, width), F32)
    results = pl.pallas_call(
        functools.partial(kernel, n_seq, n_head, float(width * n_head)),
        out_shape=(held, held, held, held),
        in_specs=[pl.BlockSpec(memory_space=pltpu.HBM)] * 8,
        out_specs=[pl.BlockSpec(memory_space=pltpu.VMEM)] * 4,
        scratch_shapes=scratch,
        compiler_params=pltpu.CompilerParams(
            collective_id=0, has_side_effects=True, vmem_limit_bytes=65800000
        ),
    )(
        queries, keys, values, gain.reshape(1, width), ridge,
        prior_gram, prior_cross, cotangent,
    )
    return pl.pallas_call(
        hand_over,
        out_shape=(shape, shape, shape, shape),
        in_specs=[pl.BlockSpec(memory_space=pltpu.VMEM)] * 4,
        out_specs=[pl.BlockSpec(memory_space=pltpu.HBM)] * 4,
        scratch_shapes=[pltpu.SemaphoreType.DMA((4,))],
        compiler_params=pltpu.CompilerParams(vmem_limit_bytes=1024 * 1024),
    )(*results)


def solution(mesh):
    in_specs = (
        P("seq", "head"),
        P("seq", "head"),
        P("seq", "head"),
        P("head"),
        P("head"),
        P("head", None, None),
        P("head", None, None),
        P("seq", "head"),
    )
    out_specs = (P("seq", "head"), P("seq", "head"), P("seq", "head"), P("seq", "head"))
    body = functools.partial(local, mesh.shape["seq"], mesh.shape["head"])
    return jax.shard_map(body, mesh=mesh, in_specs=in_specs, out_specs=out_specs, check_vma=False)
```
